512 devices in a mesh: dp: 16 (over z, core), expert: 32 (over x, y).
Axes of the slice: x: 4, y: 8, z: 8, core: 2. Of those that a mesh axis runs over, the one named last changes fastest.
Arguments:
- tokens: bfloat16 [65536, 1664], P(('dp', 'expert')), may hold values from -6 to 6
- cotangent: bfloat16 [65536, 1664], P(('dp', 'expert')), may hold values from -6 to 6
- counts: int32 [65536], P(('dp', 'expert')), may hold values from 0 to 8
- picks: int32 [16, 32, 32], P('dp'), may hold values from 0 to 4095, as said below
- router: float32 [1664, 32], replicated, may hold values from -1 to 1
- w_in: bfloat16 [32, 1664, 4096], P('expert', None, 'dp'), may hold values from -0.15625 to 0.15625
- w_out: bfloat16 [32, 4096, 1664], P('expert', 'dp'), may hold values from -0.09375 to 0.09375
Outputs:
- grad_tokens: bfloat16 [65536, 1664], P(('dp', 'expert'))
- grad_w_in: bfloat16 [32, 1664, 4096], P('expert', None, 'dp')
- grad_w_out: bfloat16 [32, 4096, 1664], P('expert', 'dp')
- grad_router: float32 [1664, 32], replicated
The draws below stay inside these ranges and needn't reach their ends.
Inputs may be any that keep to these rules, and one draw needn't show every extreme that they name: For each group and each expert, 32 distinct positions in increasing order; positions k * 128 to (k + 1) * 128 - 1 hold at most 2 of one expert's picks, and each expert takes exactly 2 from some such range in every group.
All inputs are finite; a program needn't handle non-finite values.
Results may differ from the reference program's by a relative error of at most 0.017.
Values may be sent and summed in bfloat16 or wider, within the bound.
No kernel may reach another device: no remote copies, remote signals or barrier semaphores. Data moves between devices by JAX's collectives and lax.ppermute only.
A program may use at most 64 MiB of HBM per device.

```python
import math
import jax
import jax.numpy as jnp
from jax import lax

D = 1664
FFN = 4096
SLOT = 2
TOK_DEV = 128
EXPERTS = 32
GROUP = 4096
GROUPS = 16
TOKENS = 65536
CAP = 32
N_EXPERT = 32


def draw_router(key, part):
    normal = jax.random.normal(jax.random.fold_in(key, 3), (D, EXPERTS), jnp.float32) * (2.0 / math.sqrt(D))
    normal = jnp.clip(normal, -1.0, 1.0)
    return normal


def draw_tokens(key, part):
    values = jnp.clip(jax.random.normal(jax.random.fold_in(key, 5), (TOKENS, D), jnp.float32), -6.0, 6.0)
    positions = jnp.arange(TOKENS)
    device_of = positions // TOK_DEV
    device_sign = jnp.where(jax.random.bernoulli(jax.random.fold_in(key, 11), 0.5, (TOKENS // TOK_DEV,)), 5.0, -5.0)
    spike_col = device_of % D
    columns = jnp.arange(D)
    values = jnp.where(columns[None, :] == spike_col[:, None], device_sign[device_of][:, None], values)
    return values.astype(jnp.bfloat16)


def pick_plan(key):
    base_key = jax.random.fold_in(key, 29)
    forced_count = min(8, EXPERTS)

    def one_group(group_key):
        key_perm, key_amount, key_order = jax.random.split(group_key, 3)
        perms = jax.vmap(lambda sub_key: jax.random.permutation(sub_key, N_EXPERT))(jax.random.split(key_perm, EXPERTS))
        column_ids = jnp.arange(N_EXPERT, dtype=perms.dtype)
        swapped = jnp.where(perms == 0, perms[:, 0:1], jnp.where(column_ids[None, :] == 0, 0, perms))
        forced = jnp.arange(EXPERTS)[:, None] < forced_count
        perms = jnp.where(forced, swapped, perms)
        half_count = N_EXPERT // 2
        amount = jax.random.randint(key_amount, (EXPERTS, half_count), 0, SLOT + 1)
        amount = amount.at[:, 0].set(SLOT)
        paired = jnp.concatenate([amount, SLOT - amount], axis=1)
        inverse = jnp.argsort(perms, axis=1, stable=True)
        per_source = jnp.take_along_axis(paired, inverse, axis=1)
        source_total = jnp.sum(per_source, axis=0)
        window = jnp.minimum(jnp.maximum(SLOT, (source_total + 7) // 8), TOK_DEV)
        starts = jnp.cumsum(per_source, axis=0) - per_source
        orders = jax.vmap(lambda sub_key: jax.random.permutation(sub_key, TOK_DEV))(jax.random.split(key_order, N_EXPERT))
        slot_rank = jnp.arange(SLOT, dtype=jnp.int32)
        sources = jnp.arange(N_EXPERT, dtype=jnp.int32)
        position = (starts[:, :, None] + slot_rank[None, None, :]) % window[None, :, None]
        local_pos = orders[sources[None, :, None], position]
        special = orders[0, TOK_DEV - 1]
        special_mask = forced[:, :, None] & (sources[None, :, None] == 0) & (slot_rank[None, None, :] == 0)
        local_pos = jnp.where(special_mask, special, local_pos)
        valid = slot_rank[None, None, :] < per_source[:, :, None]
        code = jnp.where(valid, sources[None, :, None] * TOK_DEV + local_pos, GROUP)
        ranked = jnp.sort(code.reshape(EXPERTS, N_EXPERT * SLOT), axis=1)[:, :CAP]
        tally = jnp.zeros((GROUP,), jnp.int32).at[ranked.reshape(-1)].add(1)
        return (ranked.astype(jnp.int32), tally)
    plans, tallies = jax.vmap(one_group)(jax.random.split(base_key, GROUPS))
    return (plans, tallies.reshape(-1))


def draw_picks(key, part):
    return pick_plan(key)[0]


def draw_counts(key, part):
    return pick_plan(key)[1]


def block_levels(own_key, dims, pieces, smallest, high):
    factor_of = 1.0
    for dim, parts in pieces:
        heights = jax.random.uniform(jax.random.fold_in(jax.random.fold_in(own_key, 6), dim), (parts,), jnp.float32, smallest / len(pieces), high / len(pieces))
        factor_of = factor_of * jnp.repeat(jnp.exp(heights), dims[dim] // parts).reshape((-1,) + (1,) * (len(dims) - 1 - dim))
    return factor_of


def gaussian(rng, shape, deviation, limit, shards=(), kind=jnp.bfloat16):
    level = block_levels(rng, shape, shards, -0.22, 0.18) if shards else 1.0
    array = jax.random.normal(rng, shape, jnp.float32) * deviation * level
    return jnp.minimum(jnp.maximum(array, -limit), limit).astype(kind)


def setup_inputs(seed: int = 0) -> dict:
    seeds = jax.random.split(jax.random.key(seed), 8)
    return {
        "tokens": draw_tokens(jax.random.fold_in(seeds[7], 71), 0),
        "cotangent": gaussian(seeds[1], (TOKENS, D), 1.0, 6.0, ((0, 512),)),
        "counts": draw_counts(jax.random.fold_in(seeds[7], 71), 0),
        "picks": draw_picks(jax.random.fold_in(seeds[7], 71), 0),
        "router": draw_router(jax.random.fold_in(seeds[7], 71), 0),
        "w_in": gaussian(seeds[5], (EXPERTS, D, FFN), D ** -0.5, 0.15625, ((0, 32), (2, 16))),
        "w_out": gaussian(seeds[6], (EXPERTS, FFN, D), FFN ** -0.5, 0.09375, ((0, 32), (1, 16))),
    }


def normal_cdf(values):
    return 0.5 * (1.0 + jax.scipy.special.erf(values * 0.7071067811865476))


def gelu_exact(values):
    return values * normal_cdf(values)


def gelu_slope(values):
    return normal_cdf(values) + values * jnp.exp(-0.5 * values * values) * 0.3989422804014327


def reference(tokens, cotangent, counts, picks, router, w_in, w_out):
    tokens_wide = tokens.astype(jnp.float32)
    logits = jnp.dot(tokens_wide, router, precision=lax.Precision.HIGHEST)
    router_prob = jax.nn.softmax(logits, axis=-1)
    weight = jnp.maximum(counts, 1).astype(jnp.float32)
    scaled = (cotangent.astype(jnp.float32) / weight[:, None]).astype(jnp.bfloat16)
    offsets = (jnp.arange(GROUPS, dtype=jnp.int32) * GROUP).astype(jnp.int32)
    pick_rows = (picks + offsets[:, None, None]).astype(jnp.int32)
    rows_by_expert = jnp.transpose(pick_rows, (1, 0, 2)).reshape(EXPERTS, GROUPS * CAP)
    block_width = FFN // GROUPS

    def per_expert(operands):
        row_index, mat_in, mat_out, expert_id = operands
        rows_x = tokens[row_index]
        rows_dy = scaled[row_index]
        gate = router_prob[row_index, expert_id].astype(jnp.bfloat16)
        pre_act = jnp.dot(rows_x, mat_in, preferred_element_type=jnp.float32)
        activated = gelu_exact(pre_act).astype(jnp.bfloat16)
        out_grad = (gate.astype(jnp.float32)[:, None] * rows_dy.astype(jnp.float32)).astype(jnp.bfloat16)
        grad_out = jnp.dot(activated.T, out_grad, preferred_element_type=jnp.float32).astype(jnp.bfloat16)
        act_grad = jnp.dot(out_grad, mat_out.T, preferred_element_type=jnp.float32)
        pre_grad = (act_grad * gelu_slope(pre_act)).astype(jnp.bfloat16)
        grad_in = jnp.dot(rows_x.T, pre_grad, preferred_element_type=jnp.float32).astype(jnp.bfloat16)
        row_sum = jnp.zeros((rows_x.shape[0], D), jnp.float32)
        gate_sum = jnp.zeros((rows_x.shape[0],), jnp.float32)
        dy_wide = rows_dy.astype(jnp.float32)
        for block_id in range(GROUPS):
            low_col = block_id * block_width
            high_col = low_col + block_width
            part_out = jnp.dot(activated[:, low_col:high_col], mat_out[low_col:high_col], preferred_element_type=jnp.float32)
            gate_sum = gate_sum + jnp.sum(dy_wide * part_out, axis=-1)
            row_part = jnp.dot(pre_grad[:, low_col:high_col], mat_in[:, low_col:high_col].T, preferred_element_type=jnp.float32)
            row_part = lax.optimization_barrier(row_part.astype(jnp.bfloat16))
            row_sum = row_sum + row_part.astype(jnp.float32)
        return grad_in, grad_out, row_sum.astype(jnp.bfloat16), gate_sum.astype(jnp.bfloat16)

    grad_w_in, grad_w_out, row_grad, gate_grad = lax.map(per_expert, (rows_by_expert, w_in, w_out, jnp.arange(EXPERTS, dtype=jnp.int32)))
    flat_rows = rows_by_expert.reshape(-1)
    expert_cols = jnp.repeat(jnp.arange(EXPERTS, dtype=jnp.int32), GROUPS * CAP)
    expert_sum = jnp.zeros((TOKENS, D), jnp.float32).at[flat_rows].add(row_grad.reshape(-1, D).astype(jnp.float32))
    prob_grad = jnp.zeros((TOKENS, EXPERTS), jnp.float32).at[flat_rows, expert_cols].add(gate_grad.reshape(-1).astype(jnp.float32))
    logit_grad = router_prob * (prob_grad - jnp.sum(router_prob * prob_grad, axis=-1, keepdims=True))
    grad_tokens = (expert_sum + jnp.dot(logit_grad, router.T, precision=lax.Precision.HIGHEST)).astype(jnp.bfloat16)
    grad_router = jnp.dot(tokens_wide.T, logit_grad, precision=lax.Precision.HIGHEST)
    return (grad_tokens, grad_w_in, grad_w_out, grad_router)
```

```python
import jax
import jax.numpy as jnp
from jax import lax
from jax.sharding import PartitionSpec as P


SLOT = 2


def dot_rows(left, right):
    return lax.dot_general(
        left, right, (((0,), (0,)), ((), ())), preferred_element_type=jnp.float32
    )


def dot_cols(left, right):
    return lax.dot_general(
        left, right, (((1,), (1,)), ((), ())), preferred_element_type=jnp.float32
    )


def dot_plain(left, right):
    return jnp.dot(left, right, preferred_element_type=jnp.float32)


def split_bf16(values, pieces):
    parts = []
    rest = values
    for _ in range(pieces):
        head = lax.reduce_precision(rest, 8, 7)
        parts.append(head.astype(jnp.bfloat16))
        rest = rest - head
    return parts


def one_hot(index, width):
    lanes = lax.broadcasted_iota(jnp.int32, (index.shape[0], width), 1)
    return (lanes == index[:, None]).astype(jnp.bfloat16)


def shards(tokens, cotangent, counts, picks, router, w_in, w_out):
    experts = lax.axis_size("expert")
    groups = lax.axis_size("dp")
    me = lax.axis_index("expert")
    tok_count, width = tokens.shape
    plan = picks[0]
    cap = plan.shape[1]
    block_in = w_in[0]
    block_out = w_out[0]

    low = me * tok_count
    inside = (plan >= low) & (plan < low + tok_count)
    held = jnp.sum(inside.astype(jnp.int32), axis=1)
    first = jnp.min(jnp.where(inside, plan, low + tok_count), axis=1) - low
    last = jnp.max(jnp.where(inside, plan, low - 1), axis=1) - low
    slot_a = jnp.where(held > 0, first, -1)
    slot_b = jnp.where(held > 1, last, -1)

    weight = jnp.maximum(counts, 1).astype(jnp.float32)
    scaled = (cotangent.astype(jnp.float32) / weight[:, None]).astype(jnp.bfloat16)
    pair = jnp.stack([slot_a, slot_b], axis=1).reshape(-1)
    send_pick = one_hot(pair, tok_count)
    send_x = dot_plain(send_pick, tokens).astype(jnp.bfloat16).reshape(experts, SLOT, width)
    send_dy = dot_plain(send_pick, scaled).astype(jnp.bfloat16).reshape(experts, SLOT, width)
    send = jnp.concatenate([send_x, send_dy], axis=1)
    recv = lax.all_to_all(send, "expert", split_axis=0, concat_axis=0, tiled=True)
    recv = recv.reshape(experts * 2 * SLOT, width)

    mine = lax.dynamic_index_in_dim(plan, me, 0, keepdims=False)
    owner = mine // tok_count
    rank = jnp.concatenate(
        [jnp.zeros((1,), jnp.int32), (owner[1:] == owner[:-1]).astype(jnp.int32)]
    )
    place_x = owner * (2 * SLOT) + rank
    pack = one_hot(jnp.concatenate([place_x, place_x + SLOT]), experts * 2 * SLOT)
    slab = dot_plain(pack, recv).astype(jnp.bfloat16)
    chips = groups // 2
    here = lax.axis_index("dp") // 2
    shape = (chips, cap, width)
    blocks_x = jnp.zeros(shape, jnp.bfloat16)
    blocks_dy = jnp.zeros(shape, jnp.bfloat16)
    up = down = slab
    for step in range(chips // 2 + 1):
        arrived = []
        if step == 0:
            arrived.append((slab, here))
        else:
            up = lax.ppermute(up, "dp", [(i, (i + 2) % groups) for i in range(groups)])
            arrived.append((up, (here - step) % chips))
            if step < chips // 2:
                down = lax.ppermute(down, "dp", [(i, (i - 2) % groups) for i in range(groups)])
                arrived.append((down, (here + step) % chips))
        for block, spot in arrived:
            blocks_x = lax.dynamic_update_slice(blocks_x, block[None, :cap], (spot, 0, 0))
            blocks_dy = lax.dynamic_update_slice(blocks_dy, block[None, cap:], (spot, 0, 0))
    swap = [(i, i ^ 1) for i in range(groups)]
    own_x = blocks_x.reshape(chips * cap, width)
    own_dy = blocks_dy.reshape(chips * cap, width)
    other_x = lax.ppermute(own_x, "dp", swap)
    other_dy = lax.ppermute(own_dy, "dp", swap)

    router_parts = split_bf16(router, 3)
    router_wide = jnp.concatenate(router_parts, axis=1)
    router_back = jnp.concatenate([router_parts[0], router_parts[0], router_parts[1]], axis=1)
    mark = (lax.broadcasted_iota(jnp.int32, (1, experts), 1) == me).astype(jnp.float32)

    def hidden_grads(rows_x, rows_dy):
        logit_parts = dot_plain(rows_x, router_wide)
        logits = (
            logit_parts[:, 2 * experts :] + logit_parts[:, experts : 2 * experts]
        ) + logit_parts[:, :experts]
        prob = jax.nn.softmax(logits, axis=-1)
        gate = jnp.sum(prob * mark, axis=-1, keepdims=True)
        pre = dot_plain(rows_x, block_in)
        cdf = 0.5 * (1.0 + lax.erf(pre * 0.7071067811865476))
        slope = cdf + pre * jnp.exp(-0.5 * pre * pre) * 0.3989422804014327
        act = (pre * cdf).astype(jnp.bfloat16)
        dy_hidden = dot_cols(rows_dy, block_out)
        gate_part = jnp.sum(act.astype(jnp.float32) * dy_hidden, axis=-1, keepdims=True)
        pre_grad = (gate * dy_hidden * slope).astype(jnp.bfloat16)
        gated = (gate * act.astype(jnp.float32)).astype(jnp.bfloat16)
        share = (gate_part * gate) * (mark - prob)
        share_hi, share_lo = split_bf16(share, 2)
        return pre_grad, gated, share_hi, share_lo

    def row_grads(pre_grad, share_hi, share_lo):
        left = jnp.concatenate([share_hi, share_lo, share_hi], axis=1)
        return dot_cols(pre_grad, block_in) + dot_cols(left, router_back)

    own_pre, own_gated, own_hi, own_lo = hidden_grads(own_x, own_dy)
    other_pre, other_gated, other_hi, other_lo = hidden_grads(other_x, other_dy)

    other_rows = row_grads(other_pre, other_hi, other_lo).astype(jnp.bfloat16)
    partner_rows = lax.ppermute(other_rows, "dp", swap)
    own_rows = row_grads(own_pre, own_hi, own_lo) + partner_rows.astype(jnp.float32)
    columns = [[i for i in range(groups) if i % 2 == core] for core in range(2)]
    pieces = lax.all_to_all(
        own_rows.astype(jnp.bfloat16).reshape(shape),
        "dp",
        split_axis=0,
        concat_axis=0,
        axis_index_groups=columns,
        tiled=True,
    )
    row_sum = jnp.sum(pieces.astype(jnp.float32), axis=0).astype(jnp.bfloat16)

    router_part = dot_rows(own_hi, own_x) + dot_rows(own_lo, own_x)
    router_part += dot_rows(other_hi, other_x) + dot_rows(other_lo, other_x)
    router_part = lax.all_to_all(
        router_part.astype(jnp.bfloat16)[:, None, :],
        "expert",
        split_axis=0,
        concat_axis=0,
        tiled=True,
    )
    router_row = jnp.sum(router_part[:, 0].astype(jnp.float32), axis=0, keepdims=True)
    router_row = lax.psum(router_row, "dp")

    grad_in = (dot_rows(own_x, own_pre) + dot_rows(other_x, other_pre)).astype(jnp.bfloat16)
    grad_out = (dot_rows(own_gated, own_dy) + dot_rows(other_gated, other_dy)).astype(jnp.bfloat16)

    spread = one_hot(place_x, experts * 2 * SLOT).reshape(cap, experts, 2, SLOT)[:, :, 0]
    back = dot_rows(spread.reshape(cap, experts * SLOT), row_sum).astype(jnp.bfloat16)
    row_hi, row_lo = split_bf16(router_row, 2)
    beside = jnp.broadcast_to(jnp.concatenate([row_hi, row_lo])[None], (experts, 2, width))
    ret = lax.all_to_all(
        jnp.concatenate([back.reshape(experts, SLOT, width), beside], axis=1),
        "expert",
        split_axis=0,
        concat_axis=0,
        tiled=True,
    )
    grad_tokens = dot_rows(send_pick, ret[:, :SLOT].reshape(experts * SLOT, width)).astype(
        jnp.bfloat16
    )
    grad_router = (ret[:, SLOT].astype(jnp.float32) + ret[:, SLOT + 1].astype(jnp.float32)).T
    return grad_tokens, grad_in[None], grad_out[None], grad_router


def solution(mesh):
    placed = (
        P(("dp", "expert"), None),
        P(("dp", "expert"), None),
        P(("dp", "expert")),
        P("dp", None, None),
        P(),
        P("expert", None, "dp"),
        P("expert", "dp", None),
    )
    return jax.shard_map(
        shards,
        mesh=mesh,
        in_specs=placed,
        out_specs=(
            P(("dp", "expert"), None),
            P("expert", None, "dp"),
            P("expert", "dp", None),
            P(),
        ),
        check_vma=False,
    )
```

```python
import jax
import jax.numpy as jnp
from jax import lax
from jax.sharding import PartitionSpec as P


SLOT = 2


def dot_rows(left, right):
    return lax.dot_general(
        left, right, (((0,), (0,)), ((), ())), preferred_element_type=jnp.float32
    )


def dot_cols(left, right):
    return lax.dot_general(
        left, right, (((1,), (1,)), ((), ())), preferred_element_type=jnp.float32
    )


def dot_plain(left, right):
    return jnp.dot(left, right, preferred_element_type=jnp.float32)


def split_bf16(values, pieces):
    parts = []
    rest = values
    for _ in range(pieces):
        head = lax.reduce_precision(rest, 8, 7)
        parts.append(head.astype(jnp.bfloat16))
        rest = rest - head
    return parts


def one_hot(index, width):
    lanes = lax.broadcasted_iota(jnp.int32, (index.shape[0], width), 1)
    return (lanes == index[:, None]).astype(jnp.bfloat16)


def grads(tokens, cotangent, counts, picks, router, w_in, w_out):
    experts = lax.axis_size("expert")
    groups = lax.axis_size("dp")
    me = lax.axis_index("expert")
    tok_count, width = tokens.shape
    plan = picks[0]
    cap = plan.shape[1]
    block_in = w_in[0]
    block_out = w_out[0]

    low = me * tok_count
    inside = (plan >= low) & (plan < low + tok_count)
    held = jnp.sum(inside.astype(jnp.int32), axis=1)
    first = jnp.min(jnp.where(inside, plan, low + tok_count), axis=1) - low
    last = jnp.max(jnp.where(inside, plan, low - 1), axis=1) - low
    slot_a = jnp.where(held > 0, first, -1)
    slot_b = jnp.where(held > 1, last, -1)

    weight = jnp.maximum(counts, 1).astype(jnp.float32)
    scaled = (cotangent.astype(jnp.float32) / weight[:, None]).astype(jnp.bfloat16)
    none = jnp.full_like(slot_a, -1)
    pick_x = one_hot(jnp.stack([slot_a, slot_b, none, none], axis=1).reshape(-1), tok_count)
    pick_dy = one_hot(jnp.stack([none, none, slot_a, slot_b], axis=1).reshape(-1), tok_count)
    send = dot_plain(pick_x, tokens) + dot_plain(pick_dy, scaled)
    send = send.astype(jnp.bfloat16).reshape(experts, 2 * SLOT, width)
    recv = lax.all_to_all(send, "expert", split_axis=0, concat_axis=0, tiled=True)
    recv = recv.reshape(experts * 2 * SLOT, width)

    mine = lax.dynamic_index_in_dim(plan, me, 0, keepdims=False)
    owner = mine // tok_count
    rank = jnp.concatenate(
        [jnp.zeros((1,), jnp.int32), (owner[1:] == owner[:-1]).astype(jnp.int32)]
    )
    place_x = owner * (2 * SLOT) + rank
    pack = one_hot(jnp.concatenate([place_x, place_x + SLOT]), experts * 2 * SLOT)
    slab = dot_plain(pack, recv).astype(jnp.bfloat16)
    chips = groups // 2
    here = lax.axis_index("dp") // 2
    core = lax.axis_index("dp") % 2
    swap = [(i, i ^ 1) for i in range(groups)]
    ring = [(i, (i + 2 - 4 * (i % 2)) % groups) for i in range(groups)]
    shape = (chips, cap, width)
    blocks = [jnp.zeros(shape, jnp.bfloat16) for _ in range(4)]

    def place(block, spot):
        for part in range(4):
            piece = block[part * cap : (part + 1) * cap][None]
            blocks[part] = lax.dynamic_update_slice(blocks[part], piece, (spot, 0, 0))

    def flip(block):
        return jnp.concatenate([block[2 * cap :], block[: 2 * cap]])

    block = jnp.concatenate([slab, lax.ppermute(slab, "dp", swap)])
    place(block, here)
    back = 2 * core - 1
    for step in range(1, chips // 2 + 1):
        block = lax.ppermute(block, "dp", ring)
        place(block, (here + back * step) % chips)
        if step < chips // 2:
            other = lax.ppermute(block, "dp", swap)
            place(flip(other), (here - back * step) % chips)
    own_x, own_dy, other_x, other_dy = (part.reshape(chips * cap, width) for part in blocks)

    router_parts = split_bf16(router, 3)
    router_wide = jnp.concatenate(router_parts, axis=1)
    router_back = jnp.concatenate([router_parts[0], router_parts[0], router_parts[1]], axis=1)
    mark = (lax.broadcasted_iota(jnp.int32, (1, experts), 1) == me).astype(jnp.float32)

    def hidden_grads(rows_x, rows_dy):
        logit_parts = dot_plain(rows_x, router_wide)
        logits = (
            logit_parts[:, 2 * experts :] + logit_parts[:, experts : 2 * experts]
        ) + logit_parts[:, :experts]
        prob = jax.nn.softmax(logits, axis=-1)
        gate = jnp.sum(prob * mark, axis=-1, keepdims=True)
        pre = dot_plain(rows_x, block_in)
        cdf = 0.5 * (1.0 + lax.erf(pre * 0.7071067811865476))
        slope = cdf + pre * jnp.exp(-0.5 * pre * pre) * 0.3989422804014327
        act = (pre * cdf).astype(jnp.bfloat16)
        dy_hidden = dot_cols(rows_dy, block_out)
        gate_part = jnp.sum(act.astype(jnp.float32) * dy_hidden, axis=-1, keepdims=True)
        pre_grad = (gate * dy_hidden * slope).astype(jnp.bfloat16)
        gated = (gate * act.astype(jnp.float32)).astype(jnp.bfloat16)
        return pre_grad, gated, gate_part, gate * (mark - prob)

    def row_grads(pre_grad, gate_part, unit):
        share_hi, share_lo = split_bf16(gate_part * unit, 2)
        left = jnp.concatenate([share_hi, share_lo, share_hi], axis=1)
        return dot_cols(pre_grad, block_in) + dot_cols(left, router_back)

    other_pre, other_gated, other_gate, other_unit = hidden_grads(other_x, other_dy)
    own_pre, own_gated, own_gate, own_unit = hidden_grads(own_x, own_dy)

    own_gate_row, other_gate_row = own_gate.reshape(1, -1), other_gate.reshape(1, -1)
    gates = jnp.concatenate(
        [
            jnp.where(core == 0, own_gate_row, other_gate_row),
            jnp.where(core == 0, other_gate_row, own_gate_row),
        ],
        axis=1,
    ).reshape(1, 2, chips * cap)
    gates = jnp.broadcast_to(gates, (groups,) + gates.shape[1:])
    gates = lax.all_to_all(gates, "dp", split_axis=0, concat_axis=0, tiled=True)
    gates = jnp.sum(gates, axis=0)
    own_total = jnp.where(core == 0, gates[0], gates[1])[:, None]
    other_total = jnp.where(core == 0, gates[1], gates[0])[:, None]

    other_rows = row_grads(other_pre, other_gate, other_unit).astype(jnp.bfloat16)
    partner_rows = lax.ppermute(other_rows, "dp", swap)
    own_rows = row_grads(own_pre, own_gate, own_unit) + partner_rows.astype(jnp.float32)
    own_rows = own_rows.astype(jnp.bfloat16).reshape(shape)
    pieces = [lax.dynamic_index_in_dim(own_rows, here, 0, keepdims=False)]
    for shift in sorted(range(1, chips), key=lambda d: -min(d, chips - d)):
        piece = lax.dynamic_index_in_dim(own_rows, (here + shift) % chips, 0, keepdims=False)
        there = [(i, (i + 2 * shift) % groups) for i in range(groups)]
        pieces.append(lax.ppermute(piece, "dp", there))
    row_sum = sum(piece.astype(jnp.float32) for piece in pieces).astype(jnp.bfloat16)

    own_hi, own_lo = split_bf16(own_total * own_unit, 2)
    other_hi, other_lo = split_bf16(other_total * other_unit, 2)
    router_part = dot_rows(own_hi, own_x) + dot_rows(own_lo, own_x)
    router_part += dot_rows(other_hi, other_x) + dot_rows(other_lo, other_x)
    router_part = router_part.astype(jnp.bfloat16)[:, None, :]
    router_part = lax.all_to_all(
        router_part, "expert", split_axis=0, concat_axis=0, tiled=True
    )
    router_row = jnp.sum(router_part[:, 0].astype(jnp.float32), axis=0, keepdims=True)

    grad_in = (dot_rows(own_x, own_pre) + dot_rows(other_x, other_pre)).astype(jnp.bfloat16)
    grad_out = (dot_rows(own_gated, own_dy) + dot_rows(other_gated, other_dy)).astype(jnp.bfloat16)

    row_hi, row_lo = split_bf16(router_row, 2)
    slot = lax.broadcasted_iota(jnp.int32, (experts * 2 * SLOT, 1), 0) % (2 * SLOT)
    back_rows = dot_rows(one_hot(place_x, experts * 2 * SLOT), row_sum)
    back_rows += jnp.where(slot == SLOT, row_hi.astype(jnp.float32), 0.0)
    back_rows += jnp.where(slot == SLOT + 1, row_lo.astype(jnp.float32), 0.0)
    ret = lax.all_to_all(
        back_rows.astype(jnp.bfloat16).reshape(experts, 2 * SLOT, width),
        "expert",
        split_axis=0,
        concat_axis=0,
        tiled=True,
    ).reshape(experts * 2 * SLOT, width)
    grad_tokens = dot_rows(pick_x, ret).astype(jnp.bfloat16)
    spot = lax.broadcasted_iota(jnp.int32, (experts, experts * 2 * SLOT), 1)
    line = lax.broadcasted_iota(jnp.int32, (experts, experts * 2 * SLOT), 0)
    halves = (spot // (2 * SLOT) == line) & (spot % (2 * SLOT) >= SLOT)
    grad_router = dot_plain(halves.astype(jnp.bfloat16), ret).T
    return grad_tokens, grad_in[None], grad_out[None], grad_router


def solution(mesh):
    placed = (
        P(("dp", "expert"), None),
        P(("dp", "expert"), None),
        P(("dp", "expert")),
        P("dp", None, None),
        P(),
        P("expert", None, "dp"),
        P("expert", "dp", None),
    )
    return jax.shard_map(
        grads,
        mesh=mesh,
        in_specs=placed,
        out_specs=(
            P(("dp", "expert"), None),
            P("expert", None, "dp"),
            P("expert", "dp", None),
            P(),
        ),
        check_vma=False,
    )
```

```python
import jax
import jax.numpy as jnp
from jax import lax
from jax.sharding import PartitionSpec as P


SLOT = 2


def dot_rows(left, right):
    return lax.dot_general(
        left, right, (((0,), (0,)), ((), ())), preferred_element_type=jnp.float32
    )


def dot_cols(left, right):
    return lax.dot_general(
        left, right, (((1,), (1,)), ((), ())), preferred_element_type=jnp.float32
    )


def dot_plain(left, right):
    return jnp.dot(left, right, preferred_element_type=jnp.float32)


def split_bf16(values, pieces):
    parts = []
    rest = values
    for _ in range(pieces):
        head = lax.reduce_precision(rest, 8, 7)
        parts.append(head.astype(jnp.bfloat16))
        rest = rest - head
    return parts


def one_hot(index, width):
    lanes = lax.broadcasted_iota(jnp.int32, (index.shape[0], width), 1)
    return (lanes == index[:, None]).astype(jnp.bfloat16)


def shards(tokens, cotangent, counts, picks, router, w_in, w_out):
    experts = lax.axis_size("expert")
    groups = lax.axis_size("dp")
    me = lax.axis_index("expert")
    tok_count, width = tokens.shape
    plan = picks[0]
    cap = plan.shape[1]
    block_in = w_in[0]
    block_out = w_out[0]

    low = me * tok_count
    inside = (plan >= low) & (plan < low + tok_count)
    held = jnp.sum(inside.astype(jnp.int32), axis=1)
    first = jnp.min(jnp.where(inside, plan, low + tok_count), axis=1) - low
    last = jnp.max(jnp.where(inside, plan, low - 1), axis=1) - low
    slot_a = jnp.where(held > 0, first, -1)
    slot_b = jnp.where(held > 1, last, -1)

    weight = jnp.maximum(counts, 1).astype(jnp.float32)
    scaled = (cotangent.astype(jnp.float32) / weight[:, None]).astype(jnp.bfloat16)
    none = jnp.full_like(slot_a, -1)
    pick_x = one_hot(jnp.stack([slot_a, slot_b, none, none], axis=1).reshape(-1), tok_count)
    pick_dy = one_hot(jnp.stack([none, none, slot_a, slot_b], axis=1).reshape(-1), tok_count)
    send = dot_plain(pick_x, tokens) + dot_plain(pick_dy, scaled)
    send = send.astype(jnp.bfloat16).reshape(experts, 2 * SLOT, width)
    recv = lax.all_to_all(send, "expert", split_axis=0, concat_axis=0, tiled=True)
    recv = recv.reshape(experts * 2 * SLOT, width)

    mine = lax.dynamic_index_in_dim(plan, me, 0, keepdims=False)
    owner = mine // tok_count
    rank = jnp.concatenate(
        [jnp.zeros((1,), jnp.int32), (owner[1:] == owner[:-1]).astype(jnp.int32)]
    )
    place_x = owner * (2 * SLOT) + rank
    pack = one_hot(jnp.concatenate([place_x, place_x + SLOT]), experts * 2 * SLOT)
    slab = dot_plain(pack, recv).astype(jnp.bfloat16)
    chips = groups // 2
    here = lax.axis_index("dp") // 2
    shape = (chips, cap, width)
    blocks_x = jnp.zeros(shape, jnp.bfloat16)
    blocks_dy = jnp.zeros(shape, jnp.bfloat16)
    up = down = slab
    for step in range(chips // 2 + 1):
        arrived = []
        if step == 0:
            arrived.append((slab, here))
        else:
            up = lax.ppermute(up, "dp", [(i, (i + 2) % groups) for i in range(groups)])
            arrived.append((up, (here - step) % chips))
            if step < chips // 2:
                down = lax.ppermute(down, "dp", [(i, (i - 2) % groups) for i in range(groups)])
                arrived.append((down, (here + step) % chips))
        for block, spot in arrived:
            blocks_x = lax.dynamic_update_slice(blocks_x, block[None, :cap], (spot, 0, 0))
            blocks_dy = lax.dynamic_update_slice(blocks_dy, block[None, cap:], (spot, 0, 0))
    swap = [(i, i ^ 1) for i in range(groups)]
    own_x = blocks_x.reshape(chips * cap, width)
    own_dy = blocks_dy.reshape(chips * cap, width)
    other_x = lax.ppermute(own_x, "dp", swap)
    other_dy = lax.ppermute(own_dy, "dp", swap)

    router_parts = split_bf16(router, 3)
    router_wide = jnp.concatenate(router_parts, axis=1)
    router_back = jnp.concatenate([router_parts[0], router_parts[0], router_parts[1]], axis=1)
    mark = (lax.broadcasted_iota(jnp.int32, (1, experts), 1) == me).astype(jnp.float32)

    def hidden_grads(rows_x, rows_dy):
        logit_parts = dot_plain(rows_x, router_wide)
        logits = (
            logit_parts[:, 2 * experts :] + logit_parts[:, experts : 2 * experts]
        ) + logit_parts[:, :experts]
        prob = jax.nn.softmax(logits, axis=-1)
        gate = jnp.sum(prob * mark, axis=-1, keepdims=True)
        pre = dot_plain(rows_x, block_in)
        cdf = 0.5 * (1.0 + lax.erf(pre * 0.7071067811865476))
        slope = cdf + pre * jnp.exp(-0.5 * pre * pre) * 0.3989422804014327
        act = (pre * cdf).astype(jnp.bfloat16)
        dy_hidden = dot_cols(rows_dy, block_out)
        gate_part = jnp.sum(act.astype(jnp.float32) * dy_hidden, axis=-1, keepdims=True)
        pre_grad = (gate * dy_hidden * slope).astype(jnp.bfloat16)
        gated = (gate * act.astype(jnp.float32)).astype(jnp.bfloat16)
        return pre_grad, gated, (gate_part * gate) * (mark - prob)

    tiles = width // 128
    deal = experts * tiles // groups

    def row_grads(pre_grad, share_hi, share_lo, extra):
        left = jnp.concatenate([share_hi, share_lo, share_hi], axis=1)
        rows = dot_cols(pre_grad, block_in) + dot_cols(left, router_back)
        return jnp.concatenate([rows, extra], axis=1)

    other_pre, other_gated, other_share = hidden_grads(other_x, other_dy)
    own_pre, own_gated, own_share = hidden_grads(own_x, own_dy)
    own_hi, own_lo = split_bf16(own_share, 2)
    other_hi, other_lo = split_bf16(other_share, 2)
    router_part = dot_rows(own_hi, own_x) + dot_rows(own_lo, own_x)
    router_part += dot_rows(other_hi, other_x) + dot_rows(other_lo, other_x)
    router_part = jnp.swapaxes(router_part.reshape(experts, tiles, 128), 0, 1)
    router_part = router_part.reshape(chips, 2, deal, 128)
    router_part = jnp.pad(router_part, ((0, 0), (0, 0), (0, cap - deal), (0, 0)))
    core = lax.axis_index("dp") % 2
    own_extra = jnp.where(core == 0, router_part[:, 0], router_part[:, 1])
    other_extra = jnp.where(core == 0, router_part[:, 1], router_part[:, 0])

    other_rows = row_grads(other_pre, other_hi, other_lo, other_extra.reshape(-1, 128))
    partner_rows = lax.ppermute(other_rows.astype(jnp.bfloat16), "dp", swap)
    own_rows = row_grads(own_pre, own_hi, own_lo, own_extra.reshape(-1, 128))
    own_rows = own_rows + partner_rows.astype(jnp.float32)
    columns = [[i for i in range(groups) if i % 2 == side] for side in range(2)]
    pieces = lax.all_to_all(
        own_rows.astype(jnp.bfloat16).reshape(chips, cap, width + 128),
        "dp",
        split_axis=0,
        concat_axis=0,
        axis_index_groups=columns,
        tiled=True,
    )
    pieces = jnp.sum(pieces.astype(jnp.float32), axis=0)
    row_sum = pieces[:, :width].astype(jnp.bfloat16)
    router_rows = pieces[:deal, width:].reshape(SLOT, width)

    grad_in = (dot_rows(own_x, own_pre) + dot_rows(other_x, other_pre)).astype(jnp.bfloat16)
    grad_out = (dot_rows(own_gated, own_dy) + dot_rows(other_gated, other_dy)).astype(jnp.bfloat16)

    slot = lax.broadcasted_iota(jnp.int32, (experts * 2 * SLOT, 1), 0) % (2 * SLOT)
    back_rows = dot_rows(one_hot(place_x, experts * 2 * SLOT), row_sum)
    for part in range(SLOT):
        back_rows += jnp.where(slot == SLOT + part, router_rows[part : part + 1], 0.0)
    ret = lax.all_to_all(
        back_rows.astype(jnp.bfloat16).reshape(experts, 2 * SLOT, width),
        "expert",
        split_axis=0,
        concat_axis=0,
        tiled=True,
    ).reshape(experts * 2 * SLOT, width)
    grad_tokens = dot_rows(pick_x, ret).astype(jnp.bfloat16)
    spot = lax.broadcasted_iota(jnp.int32, (SLOT, experts * 2 * SLOT), 1)
    line = lax.broadcasted_iota(jnp.int32, (SLOT, experts * 2 * SLOT), 0)
    router_rows = dot_plain((spot % (2 * SLOT) == SLOT + line).astype(jnp.bfloat16), ret)
    router_rows = lax.all_gather(router_rows, "dp", axis=0, tiled=True)
    router_rows = router_rows.reshape(tiles, experts, 128)
    grad_router = jnp.swapaxes(router_rows, 0, 1).reshape(experts, width).T
    return grad_tokens, grad_in[None], grad_out[None], grad_router


def solution(mesh):
    placed = (
        P(("dp", "expert"), None),
        P(("dp", "expert"), None),
        P(("dp", "expert")),
        P("dp", None, None),
        P(),
        P("expert", None, "dp"),
        P("expert", "dp", None),
    )
    return jax.shard_map(
        shards,
        mesh=mesh,
        in_specs=placed,
        out_specs=(
            P(("dp", "expert"), None),
            P("expert", None, "dp"),
            P("expert", "dp", None),
            P(),
        ),
        check_vma=False,
    )
```

```python
import jax
import jax.numpy as jnp
from jax import lax
from jax.sharding import PartitionSpec as P


SLOT = 2


def dot_rows(left, right):
    return lax.dot_general(
        left, right, (((0,), (0,)), ((), ())), preferred_element_type=jnp.float32
    )


def dot_cols(left, right):
    return lax.dot_general(
        left, right, (((1,), (1,)), ((), ())), preferred_element_type=jnp.float32
    )


def dot_plain(left, right):
    return jnp.dot(left, right, preferred_element_type=jnp.float32)


def split_bf16(values, pieces):
    parts = []
    rest = values
    for _ in range(pieces):
        head = lax.reduce_precision(rest, 8, 7)
        parts.append(head.astype(jnp.bfloat16))
        rest = rest - head
    return parts


def one_hot(index, width):
    lanes = lax.broadcasted_iota(jnp.int32, (index.shape[0], width), 1)
    return (lanes == index[:, None]).astype(jnp.bfloat16)


def grads(tokens, cotangent, counts, picks, router, w_in, w_out):
    experts = lax.axis_size("expert")
    groups = lax.axis_size("dp")
    me = lax.axis_index("expert")
    tok_count, width = tokens.shape
    plan = picks[0]
    cap = plan.shape[1]
    block_in = w_in[0]
    block_out = w_out[0]

    low = me * tok_count
    inside = (plan >= low) & (plan < low + tok_count)
    held = jnp.sum(inside.astype(jnp.int32), axis=1)
    first = jnp.min(jnp.where(inside, plan, low + tok_count), axis=1) - low
    last = jnp.max(jnp.where(inside, plan, low - 1), axis=1) - low
    slot_a = jnp.where(held > 0, first, -1)
    slot_b = jnp.where(held > 1, last, -1)

    weight = jnp.maximum(counts, 1).astype(jnp.float32)
    scaled = (cotangent.astype(jnp.float32) / weight[:, None]).astype(jnp.bfloat16)
    none = jnp.full_like(slot_a, -1)
    pick_x = one_hot(jnp.stack([slot_a, slot_b, none, none], axis=1).reshape(-1), tok_count)
    pick_dy = one_hot(jnp.stack([none, none, slot_a, slot_b], axis=1).reshape(-1), tok_count)
    send = dot_plain(pick_x, tokens) + dot_plain(pick_dy, scaled)
    send = send.astype(jnp.bfloat16).reshape(experts, 2 * SLOT, width)
    recv = lax.all_to_all(send, "expert", split_axis=0, concat_axis=0, tiled=True)
    recv = recv.reshape(experts * 2 * SLOT, width)

    mine = lax.dynamic_index_in_dim(plan, me, 0, keepdims=False)
    owner = mine // tok_count
    rank = jnp.concatenate(
        [jnp.zeros((1,), jnp.int32), (owner[1:] == owner[:-1]).astype(jnp.int32)]
    )
    place_x = owner * (2 * SLOT) + rank
    pack = one_hot(jnp.concatenate([place_x, place_x + SLOT]), experts * 2 * SLOT)
    slab = dot_plain(pack, recv).astype(jnp.bfloat16)
    chips = groups // 2
    here = lax.axis_index("dp") // 2
    shape = (chips, cap, width)
    blocks = jnp.zeros((2,) + shape, jnp.bfloat16)
    up = down = slab
    for step in range(chips // 2 + 1):
        arrived = []
        if step == 0:
            arrived.append((slab, here))
        else:
            up = lax.ppermute(up, "dp", [(i, (i + 2) % groups) for i in range(groups)])
            arrived.append((up, (here - step) % chips))
            if step < chips // 2:
                down = lax.ppermute(down, "dp", [(i, (i - 2) % groups) for i in range(groups)])
                arrived.append((down, (here + step) % chips))
        for block, spot in arrived:
            block = block.reshape(2, 1, cap, width)
            blocks = lax.dynamic_update_slice(blocks, block, (0, spot, 0, 0))
    swap = [(i, i ^ 1) for i in range(groups)]
    own = blocks.reshape(2 * chips * cap, width)
    other = lax.ppermute(own, "dp", swap)
    own_x, own_dy = own[: chips * cap], own[chips * cap :]
    other_x, other_dy = other[: chips * cap], other[chips * cap :]

    router_parts = split_bf16(router, 3)
    router_wide = jnp.concatenate(router_parts, axis=1)
    router_back = jnp.concatenate([router_parts[0], router_parts[0], router_parts[1]], axis=1)
    mark = (lax.broadcasted_iota(jnp.int32, (1, experts), 1) == me).astype(jnp.float32)

    def hidden_grads(rows_x, rows_dy):
        logit_parts = dot_plain(rows_x, router_wide)
        logits = (
            logit_parts[:, 2 * experts :] + logit_parts[:, experts : 2 * experts]
        ) + logit_parts[:, :experts]
        prob = jax.nn.softmax(logits, axis=-1)
        gate = jnp.sum(prob * mark, axis=-1, keepdims=True)
        pre = dot_plain(rows_x, block_in)
        cdf = 0.5 * (1.0 + lax.erf(pre * 0.7071067811865476))
        slope = cdf + pre * jnp.exp(-0.5 * pre * pre) * 0.3989422804014327
        act = (pre * cdf).astype(jnp.bfloat16)
        dy_hidden = dot_cols(rows_dy, block_out)
        gate_part = jnp.sum(act.astype(jnp.float32) * dy_hidden, axis=-1, keepdims=True)
        pre_grad = (gate * dy_hidden * slope).astype(jnp.bfloat16)
        gated = (gate * act.astype(jnp.float32)).astype(jnp.bfloat16)
        return pre_grad, gated, (gate_part * gate) * (mark - prob)

    tiles = width // 128
    deal = experts * tiles // groups

    def row_grads(pre_grad, share_hi, share_lo, extra):
        left = jnp.concatenate([share_hi, share_lo, share_hi], axis=1)
        rows = dot_cols(pre_grad, block_in) + dot_cols(left, router_back)
        return jnp.concatenate([rows, extra], axis=1)

    other_pre, other_gated, other_share = hidden_grads(other_x, other_dy)
    own_pre, own_gated, own_share = hidden_grads(own_x, own_dy)
    own_hi, own_lo = split_bf16(own_share, 2)
    other_hi, other_lo = split_bf16(other_share, 2)
    router_part = dot_rows(own_hi, own_x) + dot_rows(own_lo, own_x)
    router_part += dot_rows(other_hi, other_x) + dot_rows(other_lo, other_x)
    router_part = router_part.astype(jnp.bfloat16)
    router_part = jnp.concatenate(
        [router_part[:, 128 * tile : 128 * (tile + 1)] for tile in range(tiles)]
    )
    core = lax.axis_index("dp") % 2
    row_id = jnp.arange(chips * cap, dtype=jnp.int32)

    def dealt(side):
        unit = (2 * (row_id // cap) + side) * deal + row_id % cap
        pick = one_hot(jnp.where(row_id % cap < deal, unit, -1), experts * tiles)
        return dot_plain(pick, router_part)

    own_extra, other_extra = dealt(core), dealt(1 - core)

    other_rows = row_grads(other_pre, other_hi, other_lo, other_extra)
    partner_rows = lax.ppermute(other_rows.astype(jnp.bfloat16), "dp", swap)
    own_rows = row_grads(own_pre, own_hi, own_lo, own_extra)
    own_rows = own_rows + partner_rows.astype(jnp.float32)
    columns = [[i for i in range(groups) if i % 2 == side] for side in range(2)]
    pieces = lax.all_to_all(
        own_rows.astype(jnp.bfloat16).reshape(chips, cap, width + 128),
        "dp",
        split_axis=0,
        concat_axis=0,
        axis_index_groups=columns,
        tiled=True,
    )
    pieces = jnp.sum(pieces.astype(jnp.float32), axis=0)
    row_sum = pieces[:, :width].astype(jnp.bfloat16)
    router_rows = pieces[:deal, width:].reshape(SLOT, width)

    grad_in = (dot_rows(own_x, own_pre) + dot_rows(other_x, other_pre)).astype(jnp.bfloat16)
    grad_out = (dot_rows(own_gated, own_dy) + dot_rows(other_gated, other_dy)).astype(jnp.bfloat16)

    slot = lax.broadcasted_iota(jnp.int32, (experts * 2 * SLOT, 1), 0) % (2 * SLOT)
    back_rows = dot_rows(one_hot(place_x, experts * 2 * SLOT), row_sum)
    for part in range(SLOT):
        back_rows += jnp.where(slot == SLOT + part, router_rows[part : part + 1], 0.0)
    ret = lax.all_to_all(
        back_rows.astype(jnp.bfloat16).reshape(experts, 2 * SLOT, width),
        "expert",
        split_axis=0,
        concat_axis=0,
        tiled=True,
    ).reshape(experts * 2 * SLOT, width)
    grad_tokens = dot_rows(pick_x, ret).astype(jnp.bfloat16)
    spot = lax.broadcasted_iota(jnp.int32, (SLOT, experts * 2 * SLOT), 1)
    line = lax.broadcasted_iota(jnp.int32, (SLOT, experts * 2 * SLOT), 0)
    router_rows = dot_plain((spot % (2 * SLOT) == SLOT + line).astype(jnp.bfloat16), ret)
    router_rows = jnp.broadcast_to(router_rows[None], (groups, SLOT, width))
    router_rows = lax.all_to_all(router_rows, "dp", split_axis=0, concat_axis=0, tiled=True)
    router_rows = router_rows.reshape(tiles, experts, 128)
    grad_router = jnp.swapaxes(router_rows, 0, 1).reshape(experts, width).T
    return grad_tokens, grad_in[None], grad_out[None], grad_router


def solution(mesh):
    placed = (
        P(("dp", "expert"), None),
        P(("dp", "expert"), None),
        P(("dp", "expert")),
        P("dp", None, None),
        P(),
        P("expert", None, "dp"),
        P("expert", "dp", None),
    )
    return jax.shard_map(
        grads,
        mesh=mesh,
        in_specs=placed,
        out_specs=(
            P(("dp", "expert"), None),
            P("expert", None, "dp"),
            P("expert", "dp", None),
            P(),
        ),
        check_vma=False,
    )
```

```python
import jax
import jax.numpy as jnp
from jax import lax
from jax.sharding import PartitionSpec as P


SLOT = 2


def dot_rows(left, right):
    return lax.dot_general(
        left, right, (((0,), (0,)), ((), ())), preferred_element_type=jnp.float32
    )


def dot_cols(left, right):
    return lax.dot_general(
        left, right, (((1,), (1,)), ((), ())), preferred_element_type=jnp.float32
    )


def dot_plain(left, right):
    return jnp.dot(left, right, preferred_element_type=jnp.float32)


def split_bf16(values, pieces):
    parts = []
    rest = values
    for _ in range(pieces):
        head = lax.reduce_precision(rest, 8, 7)
        parts.append(head.astype(jnp.bfloat16))
        rest = rest - head
    return parts


def one_hot(index, width):
    lanes = lax.broadcasted_iota(jnp.int32, (index.shape[0], width), 1)
    return (lanes == index[:, None]).astype(jnp.bfloat16)


def grads(tokens, cotangent, counts, picks, router, w_in, w_out):
    experts = lax.axis_size("expert")
    groups = lax.axis_size("dp")
    me = lax.axis_index("expert")
    tok_count, width = tokens.shape
    plan = picks[0]
    cap = plan.shape[1]
    block_in = w_in[0]
    block_out = w_out[0]

    low = me * tok_count
    inside = (plan >= low) & (plan < low + tok_count)
    held = jnp.sum(inside.astype(jnp.int32), axis=1)
    first = jnp.min(jnp.where(inside, plan, low + tok_count), axis=1) - low
    last = jnp.max(jnp.where(inside, plan, low - 1), axis=1) - low
    slot_a = jnp.where(held > 0, first, -1)
    slot_b = jnp.where(held > 1, last, -1)

    weight = jnp.maximum(counts, 1).astype(jnp.float32)
    scaled = (cotangent.astype(jnp.float32) / weight[:, None]).astype(jnp.bfloat16)
    none = jnp.full_like(slot_a, -1)
    pick_x = one_hot(jnp.stack([slot_a, slot_b, none, none], axis=1).reshape(-1), tok_count)
    pick_dy = one_hot(jnp.stack([none, none, slot_a, slot_b], axis=1).reshape(-1), tok_count)
    send = dot_plain(pick_x, tokens) + dot_plain(pick_dy, scaled)
    send = send.astype(jnp.bfloat16).reshape(experts, 2 * SLOT, width)
    recv = lax.all_to_all(send, "expert", split_axis=0, concat_axis=0, tiled=True)
    recv = recv.reshape(experts * 2 * SLOT, width)

    mine = lax.dynamic_index_in_dim(plan, me, 0, keepdims=False)
    owner = mine // tok_count
    rank = jnp.concatenate(
        [jnp.zeros((1,), jnp.int32), (owner[1:] == owner[:-1]).astype(jnp.int32)]
    )
    place_x = owner * (2 * SLOT) + rank
    pack = one_hot(jnp.concatenate([place_x, place_x + SLOT]), experts * 2 * SLOT)
    slab = dot_plain(pack, recv).astype(jnp.bfloat16)
    chips = groups // 2
    here = lax.axis_index("dp") // 2
    shape = (chips, cap, width)
    blocks_x = jnp.zeros(shape, jnp.bfloat16)
    blocks_dy = jnp.zeros(shape, jnp.bfloat16)
    up = down = slab
    for step in range(chips // 2 + 1):
        arrived = []
        if step == 0:
            arrived.append((slab, here))
        else:
            up = lax.ppermute(up, "dp", [(i, (i + 2) % groups) for i in range(groups)])
            arrived.append((up, (here - step) % chips))
            if step < chips // 2:
                down = lax.ppermute(down, "dp", [(i, (i - 2) % groups) for i in range(groups)])
                arrived.append((down, (here + step) % chips))
        for block, spot in arrived:
            blocks_x = lax.dynamic_update_slice(blocks_x, block[None, :cap], (spot, 0, 0))
            blocks_dy = lax.dynamic_update_slice(blocks_dy, block[None, cap:], (spot, 0, 0))
    swap = [(i, i ^ 1) for i in range(groups)]
    own_x = blocks_x.reshape(chips * cap, width)
    own_dy = blocks_dy.reshape(chips * cap, width)
    other_x = lax.ppermute(own_x, "dp", swap)
    other_dy = lax.ppermute(own_dy, "dp", swap)

    router_parts = split_bf16(router, 3)
    router_wide = jnp.concatenate(router_parts, axis=1)
    router_back = jnp.concatenate([router_parts[0], router_parts[0], router_parts[1]], axis=1)
    mark = (lax.broadcasted_iota(jnp.int32, (1, experts), 1) == me).astype(jnp.float32)

    def hidden_grads(rows_x, rows_dy):
        logit_parts = dot_plain(rows_x, router_wide)
        logits = (
            logit_parts[:, 2 * experts :] + logit_parts[:, experts : 2 * experts]
        ) + logit_parts[:, :experts]
        prob = jax.nn.softmax(logits, axis=-1)
        gate = jnp.sum(prob * mark, axis=-1, keepdims=True)
        pre = dot_plain(rows_x, block_in)
        cdf = 0.5 * (1.0 + lax.erf(pre * 0.7071067811865476))
        slope = cdf + pre * jnp.exp(-0.5 * pre * pre) * 0.3989422804014327
        act = (pre * cdf).astype(jnp.bfloat16)
        dy_hidden = dot_cols(rows_dy, block_out)
        gate_part = jnp.sum(act.astype(jnp.float32) * dy_hidden, axis=-1, keepdims=True)
        pre_grad = (gate * dy_hidden * slope).astype(jnp.bfloat16)
        gated = (gate * act.astype(jnp.float32)).astype(jnp.bfloat16)
        return pre_grad, gated, (gate_part * gate) * (mark - prob)

    tiles = width // 128
    deal = experts * tiles // groups

    def row_grads(pre_grad, share_hi, share_lo, extra):
        left = jnp.concatenate([share_hi, share_lo, share_hi], axis=1)
        rows = dot_cols(pre_grad, block_in) + dot_cols(left, router_back)
        return jnp.concatenate([rows, extra], axis=1)

    other_pre, other_gated, other_share = hidden_grads(other_x, other_dy)
    own_pre, own_gated, own_share = hidden_grads(own_x, own_dy)
    own_hi, own_lo = split_bf16(own_share, 2)
    other_hi, other_lo = split_bf16(other_share, 2)
    router_part = dot_rows(own_hi, own_x) + dot_rows(own_lo, own_x)
    router_part += dot_rows(other_hi, other_x) + dot_rows(other_lo, other_x)
    router_part = router_part.astype(jnp.bfloat16)
    router_part = jnp.concatenate(
        [router_part[:, 128 * tile : 128 * (tile + 1)] for tile in range(tiles)]
    )
    core = lax.axis_index("dp") % 2
    row_id = jnp.arange(chips * cap, dtype=jnp.int32)

    def dealt(side):
        group, spot = 2 * (row_id // cap) + side, row_id % cap
        unit = spot % tiles * experts + SLOT * group + spot // tiles
        pick = one_hot(jnp.where(row_id % cap < deal, unit, -1), experts * tiles)
        return dot_plain(pick, router_part)

    own_extra, other_extra = dealt(core), dealt(1 - core)

    other_rows = row_grads(other_pre, other_hi, other_lo, other_extra)
    partner_rows = lax.ppermute(other_rows.astype(jnp.bfloat16), "dp", swap)
    own_rows = row_grads(own_pre, own_hi, own_lo, own_extra)
    own_rows = own_rows + partner_rows.astype(jnp.float32)
    columns = [[i for i in range(groups) if i % 2 == side] for side in range(2)]
    own_rows = own_rows.astype(jnp.bfloat16).reshape(chips, cap, width + 128)
    pieces = lax.all_to_all(
        own_rows,
        "dp",
        split_axis=0,
        concat_axis=0,
        axis_index_groups=columns,
        tiled=True,
    )
    router_rows = jnp.sum(pieces[:, :deal, width:].astype(jnp.float32), axis=0)
    router_rows = router_rows.reshape(SLOT, width)

    grad_in = dot_rows(own_x, own_pre) + dot_rows(other_x, other_pre)
    grad_out = dot_rows(own_gated, own_dy) + dot_rows(other_gated, other_dy)
    grad_in, grad_out = grad_in.astype(jnp.bfloat16), grad_out.astype(jnp.bfloat16)

    slot = lax.broadcasted_iota(jnp.int32, (experts * 2 * SLOT, 1), 0) % (2 * SLOT)
    spread = one_hot(jnp.tile(place_x, chips), experts * 2 * SLOT)
    back_rows = dot_rows(spread, pieces[:, :, :width].reshape(chips * cap, width))
    for part in range(SLOT):
        back_rows += jnp.where(slot == SLOT + part, router_rows[part : part + 1], 0.0)
    ret = lax.all_to_all(
        back_rows.astype(jnp.bfloat16).reshape(experts, 2 * SLOT, width),
        "expert",
        split_axis=0,
        concat_axis=0,
        tiled=True,
    )
    router_rows = jnp.sum(ret[:, SLOT:].astype(jnp.float32), axis=0)
    grad_tokens = dot_rows(pick_x, ret.reshape(experts * 2 * SLOT, width)).astype(jnp.bfloat16)
    router_rows = jnp.broadcast_to(router_rows[None], (groups, SLOT, width))
    router_rows = lax.all_to_all(router_rows, "dp", split_axis=0, concat_axis=0, tiled=True)
    grad_router = router_rows.reshape(experts, width).T
    return grad_tokens, grad_in[None], grad_out[None], grad_router


def solution(mesh):
    placed = (
        P(("dp", "expert"), None),
        P(("dp", "expert"), None),
        P(("dp", "expert")),
        P("dp", None, None),
        P(),
        P("expert", None, "dp"),
        P("expert", "dp", None),
    )
    return jax.shard_map(
        grads,
        mesh=mesh,
        in_specs=placed,
        out_specs=(
            P(("dp", "expert"), None),
            P("expert", None, "dp"),
            P("expert", "dp", None),
            P(),
        ),
        check_vma=False,
    )
```

```python
import jax
import jax.numpy as jnp
from jax import lax
from jax.sharding import PartitionSpec as P


SLOT = 2


def dot_rows(left, right):
    return lax.dot_general(
        left, right, (((0,), (0,)), ((), ())), preferred_element_type=jnp.float32
    )


def dot_cols(left, right):
    return lax.dot_general(
        left, right, (((1,), (1,)), ((), ())), preferred_element_type=jnp.float32
    )


def dot_plain(left, right):
    return jnp.dot(left, right, preferred_element_type=jnp.float32)


def split_bf16(values, pieces):
    parts = []
    rest = values
    for _ in range(pieces):
        head = lax.reduce_precision(rest, 8, 7)
        parts.append(head.astype(jnp.bfloat16))
        rest = rest - head
    return parts


def one_hot(index, width):
    lanes = lax.broadcasted_iota(jnp.int32, (index.shape[0], width), 1)
    return (lanes == index[:, None]).astype(jnp.bfloat16)


def grads(tokens, cotangent, counts, picks, router, w_in, w_out):
    experts = lax.axis_size("expert")
    groups = lax.axis_size("dp")
    me = lax.axis_index("expert")
    tok_count, width = tokens.shape
    plan = picks[0]
    cap = plan.shape[1]
    block_in = w_in[0]
    block_out = w_out[0]

    low = me * tok_count
    inside = (plan >= low) & (plan < low + tok_count)
    held = jnp.sum(inside.astype(jnp.int32), axis=1)
    first = jnp.min(jnp.where(inside, plan, low + tok_count), axis=1) - low
    last = jnp.max(jnp.where(inside, plan, low - 1), axis=1) - low
    slot_a = jnp.where(held > 0, first, -1)
    slot_b = jnp.where(held > 1, last, -1)

    weight = jnp.maximum(counts, 1).astype(jnp.float32)
    scaled = (cotangent.astype(jnp.float32) / weight[:, None]).astype(jnp.bfloat16)
    none = jnp.full_like(slot_a, -1)
    pick_x = one_hot(jnp.stack([slot_a, slot_b, none, none], axis=1).reshape(-1), tok_count)
    pick_dy = one_hot(jnp.stack([none, none, slot_a, slot_b], axis=1).reshape(-1), tok_count)
    send = dot_plain(pick_x, tokens) + dot_plain(pick_dy, scaled)
    send = send.astype(jnp.bfloat16).reshape(experts, 2 * SLOT, width)
    recv = lax.all_to_all(send, "expert", split_axis=0, concat_axis=0, tiled=True)
    recv = recv.reshape(experts * 2 * SLOT, width)

    mine = lax.dynamic_index_in_dim(plan, me, 0, keepdims=False)
    owner = mine // tok_count
    rank = jnp.concatenate(
        [jnp.zeros((1,), jnp.int32), (owner[1:] == owner[:-1]).astype(jnp.int32)]
    )
    place_x = owner * (2 * SLOT) + rank
    pack = one_hot(jnp.concatenate([place_x, place_x + SLOT]), experts * 2 * SLOT)
    slab = dot_plain(pack, recv).astype(jnp.bfloat16)
    swap = [(i, i ^ 1) for i in range(groups)]
    partner_in = lax.ppermute(block_in, "dp", swap)
    partner_out = lax.ppermute(block_out, "dp", swap)

    chips = groups // 2
    here = lax.axis_index("dp") // 2
    shape = (chips, cap, width)
    blocks_x = jnp.zeros(shape, jnp.bfloat16)
    blocks_dy = jnp.zeros(shape, jnp.bfloat16)
    core = lax.axis_index("dp") % 2
    toward = 2 * core - 1
    first_hop = [(i, (i + 2 - 4 * (i % 2)) % groups) for i in range(groups)]
    second_hop = [(i, (i - 2 + 4 * (i % 2)) % groups) for i in range(groups)]
    first = second = slab
    for step in range(chips // 2 + 1):
        arrived = []
        if step == 0:
            arrived.append((slab, here))
        else:
            first = lax.ppermute(first, "dp", first_hop)
            arrived.append((first, (here + toward * step) % chips))
            if step < chips // 2:
                second = lax.ppermute(second, "dp", second_hop)
                arrived.append((second, (here - toward * step) % chips))
        for block, spot in arrived:
            blocks_x = lax.dynamic_update_slice(blocks_x, block[None, :cap], (spot, 0, 0))
            blocks_dy = lax.dynamic_update_slice(blocks_dy, block[None, cap:], (spot, 0, 0))
    rows_x = blocks_x.reshape(chips * cap, width)
    rows_dy = blocks_dy.reshape(chips * cap, width)

    router_parts = split_bf16(router, 3)
    router_wide = jnp.concatenate(router_parts, axis=1)
    router_back = jnp.concatenate([router_parts[0], router_parts[0], router_parts[1]], axis=1)
    mark = (lax.broadcasted_iota(jnp.int32, (1, experts), 1) == me).astype(jnp.float32)

    logit_parts = dot_plain(rows_x, router_wide)
    logits = (
        logit_parts[:, 2 * experts :] + logit_parts[:, experts : 2 * experts]
    ) + logit_parts[:, :experts]
    prob = jax.nn.softmax(logits, axis=-1)
    gate = jnp.sum(prob * mark, axis=-1, keepdims=True)

    def hidden_grads(mat_in, mat_out):
        pre = dot_plain(rows_x, mat_in)
        cdf = 0.5 * (1.0 + lax.erf(pre * 0.7071067811865476))
        slope = cdf + pre * jnp.exp(-0.5 * pre * pre) * 0.3989422804014327
        act = (pre * cdf).astype(jnp.bfloat16)
        dy_hidden = dot_cols(rows_dy, mat_out)
        gate_part = jnp.sum(act.astype(jnp.float32) * dy_hidden, axis=-1, keepdims=True)
        pre_grad = (gate * dy_hidden * slope).astype(jnp.bfloat16)
        gated = (gate * act.astype(jnp.float32)).astype(jnp.bfloat16)
        return pre_grad, gated, gate_part

    own_pre, own_gated, own_gate = hidden_grads(block_in, block_out)
    other_pre, other_gated, other_gate = hidden_grads(partner_in, partner_out)
    gate_part = own_gate + other_gate

    share_hi, share_lo = split_bf16((gate_part * gate) * (mark - prob), 2)

    tiles = width // 128
    deal = experts * tiles // groups
    row_id = jnp.arange(chips * cap, dtype=jnp.int32)
    router_part = dot_rows(share_hi, rows_x) + dot_rows(share_lo, rows_x)
    router_part = router_part.astype(jnp.bfloat16)
    router_part = jnp.concatenate(
        [router_part[:, 128 * tile : 128 * (tile + 1)] for tile in range(tiles)]
    )

    def dealt(side):
        group, spot = 2 * (row_id // cap) + side, row_id % cap
        unit = spot % tiles * experts + SLOT * group + spot // tiles
        pick = one_hot(jnp.where(spot < deal, unit, -1), experts * tiles)
        return dot_plain(pick, router_part)

    partner_extra = lax.ppermute(dealt(1 - core).astype(jnp.bfloat16), "dp", swap)
    extra = (dealt(core) + partner_extra.astype(jnp.float32)).astype(jnp.bfloat16)

    left = jnp.concatenate([share_hi, share_lo, share_hi], axis=1)
    rows = dot_cols(own_pre, block_in) + dot_cols(other_pre, partner_in)
    rows = (rows + dot_cols(left, router_back)).astype(jnp.bfloat16)
    rows = jnp.concatenate([rows, extra], axis=1).reshape(chips, cap, width + 128)
    columns = [[i for i in range(groups) if i % 2 == side] for side in range(2)]
    pieces = lax.all_to_all(
        rows,
        "dp",
        split_axis=0,
        concat_axis=0,
        axis_index_groups=columns,
        tiled=True,
    )
    router_rows = jnp.sum(pieces[:, :deal, width:].astype(jnp.float32), axis=0)
    router_rows = router_rows.reshape(SLOT, width)

    trade_in = dot_rows(rows_x, other_pre).astype(jnp.bfloat16)
    trade_out = dot_rows(other_gated, rows_dy).astype(jnp.bfloat16)
    trade_in = lax.ppermute(trade_in, "dp", swap)
    trade_out = lax.ppermute(trade_out, "dp", swap)
    grad_in = dot_rows(rows_x, own_pre) + trade_in.astype(jnp.float32)
    grad_out = dot_rows(own_gated, rows_dy) + trade_out.astype(jnp.float32)
    grad_in, grad_out = grad_in.astype(jnp.bfloat16), grad_out.astype(jnp.bfloat16)

    slot = lax.broadcasted_iota(jnp.int32, (experts * 2 * SLOT, 1), 0) % (2 * SLOT)
    spread = one_hot(jnp.tile(place_x, chips), experts * 2 * SLOT)
    back_rows = dot_rows(spread, pieces[:, :, :width].reshape(chips * cap, width))
    for part in range(SLOT):
        back_rows += jnp.where(slot == SLOT + part, router_rows[part : part + 1], 0.0)
    ret = lax.all_to_all(
        back_rows.astype(jnp.bfloat16).reshape(experts, 2 * SLOT, width),
        "expert",
        split_axis=0,
        concat_axis=0,
        tiled=True,
    )
    router_rows = jnp.sum(ret[:, SLOT:].astype(jnp.float32), axis=0)
    grad_tokens = dot_rows(pick_x, ret.reshape(experts * 2 * SLOT, width)).astype(jnp.bfloat16)
    router_rows = router_rows.astype(jnp.bfloat16)
    router_rows = jnp.broadcast_to(router_rows[None], (groups, SLOT, width))
    router_rows = lax.all_to_all(router_rows, "dp", split_axis=0, concat_axis=0, tiled=True)
    grad_router = router_rows.reshape(experts, width).astype(jnp.float32).T
    return grad_tokens, grad_in[None], grad_out[None], grad_router


def solution(mesh):
    placed = (
        P(("dp", "expert"), None),
        P(("dp", "expert"), None),
        P(("dp", "expert")),
        P("dp", None, None),
        P(),
        P("expert", None, "dp"),
        P("expert", "dp", None),
    )
    return jax.shard_map(
        grads,
        mesh=mesh,
        in_specs=placed,
        out_specs=(
            P(("dp", "expert"), None),
            P("expert", None, "dp"),
            P("expert", "dp", None),
            P(),
        ),
        check_vma=False,
    )
```

```python
import jax
import jax.numpy as jnp
from jax import lax
from jax.sharding import PartitionSpec as P


SLOT = 2


def dot_rows(left, right):
    return lax.dot_general(
        left, right, (((0,), (0,)), ((), ())), preferred_element_type=jnp.float32
    )


def dot_cols(left, right):
    return lax.dot_general(
        left, right, (((1,), (1,)), ((), ())), preferred_element_type=jnp.float32
    )


def dot_plain(left, right):
    return jnp.dot(left, right, preferred_element_type=jnp.float32)


def split_bf16(values, pieces):
    parts = []
    rest = values
    for _ in range(pieces):
        head = lax.reduce_precision(rest, 8, 7)
        parts.append(head.astype(jnp.bfloat16))
        rest = rest - head
    return parts


def one_hot(index, width):
    lanes = lax.broadcasted_iota(jnp.int32, (index.shape[0], width), 1)
    return (lanes == index[:, None]).astype(jnp.bfloat16)


def grads(tokens, cotangent, counts, picks, router, w_in, w_out):
    experts = lax.axis_size("expert")
    groups = lax.axis_size("dp")
    me = lax.axis_index("expert")
    tok_count, width = tokens.shape
    plan = picks[0]
    cap = plan.shape[1]
    hidden = w_in.shape[2]
    block_in = w_in[0]
    block_out = w_out[0]

    low = me * tok_count
    inside = (plan >= low) & (plan < low + tok_count)
    held = jnp.sum(inside.astype(jnp.int32), axis=1)
    first = jnp.min(jnp.where(inside, plan, low + tok_count), axis=1) - low
    last = jnp.max(jnp.where(inside, plan, low - 1), axis=1) - low
    slot_a = jnp.where(held > 0, first, -1)
    slot_b = jnp.where(held > 1, last, -1)

    weight = jnp.maximum(counts, 1).astype(jnp.float32)
    scaled = (cotangent.astype(jnp.float32) / weight[:, None]).astype(jnp.bfloat16)
    none = jnp.full_like(slot_a, -1)
    pick_x = one_hot(jnp.stack([slot_a, slot_b, none, none], axis=1).reshape(-1), tok_count)
    pick_dy = one_hot(jnp.stack([none, none, slot_a, slot_b], axis=1).reshape(-1), tok_count)
    send = dot_plain(pick_x, tokens) + dot_plain(pick_dy, scaled)
    send = send.astype(jnp.bfloat16).reshape(experts, 2 * SLOT, width)
    recv = lax.all_to_all(send, "expert", split_axis=0, concat_axis=0, tiled=True)
    recv = recv.reshape(experts * 2 * SLOT, width)

    mine = lax.dynamic_index_in_dim(plan, me, 0, keepdims=False)
    owner = mine // tok_count
    rank = jnp.concatenate(
        [jnp.zeros((1,), jnp.int32), (owner[1:] == owner[:-1]).astype(jnp.int32)]
    )
    place_x = owner * (2 * SLOT) + rank
    pack = one_hot(jnp.concatenate([place_x, place_x + SLOT]), experts * 2 * SLOT)
    slab = dot_plain(pack, recv).astype(jnp.bfloat16)
    swap = [(i, i ^ 1) for i in range(groups)]
    partner_in = lax.ppermute(block_in, "dp", swap)
    partner_out = lax.ppermute(block_out, "dp", swap)
    both_in = jnp.concatenate([block_in, partner_in], axis=1)
    both_out = jnp.concatenate([block_out, partner_out])
    both_in, both_out = lax.optimization_barrier((both_in, both_out))

    chips = groups // 2
    here = lax.axis_index("dp") // 2
    shape = (chips, cap, width)
    blocks_x = jnp.zeros(shape, jnp.bfloat16)
    blocks_dy = jnp.zeros(shape, jnp.bfloat16)
    up = down = slab
    for step in range(chips // 2 + 1):
        arrived = []
        if step == 0:
            arrived.append((slab, here))
        else:
            if step == chips // 2:
                early_x, early_dy = blocks_x, blocks_dy
            up = lax.ppermute(up, "dp", [(i, (i + 2) % groups) for i in range(groups)])
            arrived.append((up, (here - step) % chips))
            if step < chips // 2:
                down = lax.ppermute(down, "dp", [(i, (i - 2) % groups) for i in range(groups)])
                arrived.append((down, (here + step) % chips))
        for block, spot in arrived:
            blocks_x = lax.dynamic_update_slice(blocks_x, block[None, :cap], (spot, 0, 0))
            blocks_dy = lax.dynamic_update_slice(blocks_dy, block[None, cap:], (spot, 0, 0))
    router_parts = split_bf16(router, 3)
    router_wide = jnp.concatenate(router_parts, axis=1)
    router_back = jnp.concatenate([router_parts[0], router_parts[0], router_parts[1]], axis=1)
    mark = (lax.broadcasted_iota(jnp.int32, (1, experts), 1) == me).astype(jnp.float32)

    def hidden_grads(rows_x, rows_dy):
        logit_parts = dot_plain(rows_x, router_wide)
        logits = (
            logit_parts[:, 2 * experts :] + logit_parts[:, experts : 2 * experts]
        ) + logit_parts[:, :experts]
        prob = jax.nn.softmax(logits, axis=-1)
        gate = jnp.sum(prob * mark, axis=-1, keepdims=True)
        pre = dot_plain(rows_x, both_in)
        cdf = 0.5 * (1.0 + lax.erf(pre * 0.7071067811865476))
        slope = cdf + pre * jnp.exp(-0.5 * pre * pre) * 0.3989422804014327
        act = (pre * cdf).astype(jnp.bfloat16)
        dy_hidden = dot_cols(rows_dy, both_out)
        gate_part = jnp.sum(act.astype(jnp.float32) * dy_hidden, axis=-1, keepdims=True)
        pre_grad = (gate * dy_hidden * slope).astype(jnp.bfloat16)
        gated = (gate * act.astype(jnp.float32)).astype(jnp.bfloat16)

        share_hi, share_lo = split_bf16((gate_part * gate) * (mark - prob), 2)
        return pre_grad, gated, share_hi, share_lo

    rows_x = blocks_x.reshape(chips * cap, width)
    rows_dy = blocks_dy.reshape(chips * cap, width)
    early = hidden_grads(early_x.reshape(chips * cap, width), early_dy.reshape(chips * cap, width))
    late = hidden_grads(up[:cap], up[cap:])
    hole = (here - chips // 2) % chips * cap
    pre_grad, gated, share_hi, share_lo = (
        lax.dynamic_update_slice(most, rest, (hole, 0)) for most, rest in zip(early, late)
    )

    tiles = width // 128
    deal = experts * tiles // groups
    core = lax.axis_index("dp") % 2
    row_id = jnp.arange(chips * cap, dtype=jnp.int32)
    router_part = dot_rows(share_hi, rows_x) + dot_rows(share_lo, rows_x)
    router_part = router_part.astype(jnp.bfloat16)
    router_part = jnp.concatenate(
        [router_part[:, 128 * tile : 128 * (tile + 1)] for tile in range(tiles)]
    )

    def dealt(side):
        group, spot = 2 * (row_id // cap) + side, row_id % cap
        unit = spot % tiles * experts + SLOT * group + spot // tiles
        pick = one_hot(jnp.where(spot < deal, unit, -1), experts * tiles)
        return dot_plain(pick, router_part)

    partner_extra = lax.ppermute(dealt(1 - core).astype(jnp.bfloat16), "dp", swap)
    extra = (dealt(core) + partner_extra.astype(jnp.float32)).astype(jnp.bfloat16)

    left = jnp.concatenate([share_hi, share_lo, share_hi], axis=1)
    rows = (dot_cols(pre_grad, both_in) + dot_cols(left, router_back)).astype(jnp.bfloat16)
    rows = jnp.concatenate([rows, extra], axis=1).reshape(chips, cap, width + 128)
    columns = [[i for i in range(groups) if i % 2 == side] for side in range(2)]
    pieces = lax.all_to_all(
        rows,
        "dp",
        split_axis=0,
        concat_axis=0,
        axis_index_groups=columns,
        tiled=True,
    )
    router_rows = jnp.sum(pieces[:, :deal, width:].astype(jnp.float32), axis=0)
    router_rows = router_rows.reshape(SLOT, width)

    partner_in = dot_rows(rows_x, pre_grad[:, hidden:]).astype(jnp.bfloat16)
    partner_out = dot_rows(gated[:, hidden:], rows_dy).astype(jnp.bfloat16)
    partner_in = lax.ppermute(partner_in, "dp", swap)
    partner_out = lax.ppermute(partner_out, "dp", swap)
    grad_in = dot_rows(rows_x, pre_grad[:, :hidden]) + partner_in.astype(jnp.float32)
    grad_out = dot_rows(gated[:, :hidden], rows_dy) + partner_out.astype(jnp.float32)
    grad_in, grad_out = grad_in.astype(jnp.bfloat16), grad_out.astype(jnp.bfloat16)

    slot = lax.broadcasted_iota(jnp.int32, (experts * 2 * SLOT, 1), 0) % (2 * SLOT)
    spread = one_hot(jnp.tile(place_x, chips), experts * 2 * SLOT)
    back_rows = dot_rows(spread, pieces[:, :, :width].reshape(chips * cap, width))
    for part in range(SLOT):
        back_rows += jnp.where(slot == SLOT + part, router_rows[part : part + 1], 0.0)
    ret = lax.all_to_all(
        back_rows.astype(jnp.bfloat16).reshape(experts, 2 * SLOT, width),
        "expert",
        split_axis=0,
        concat_axis=0,
        tiled=True,
    )
    router_rows = jnp.sum(ret[:, SLOT:].astype(jnp.float32), axis=0)
    grad_tokens = dot_rows(pick_x, ret.reshape(experts * 2 * SLOT, width)).astype(jnp.bfloat16)
    router_rows = router_rows.astype(jnp.bfloat16)
    router_rows = jnp.broadcast_to(router_rows[None], (groups, SLOT, width))
    router_rows = lax.all_to_all(router_rows, "dp", split_axis=0, concat_axis=0, tiled=True)
    grad_router = router_rows.reshape(experts, width).astype(jnp.float32).T
    return grad_tokens, grad_in[None], grad_out[None], grad_router


def solution(mesh):
    placed = (
        P(("dp", "expert"), None),
        P(("dp", "expert"), None),
        P(("dp", "expert")),
        P("dp", None, None),
        P(),
        P("expert", None, "dp"),
        P("expert", "dp", None),
    )
    return jax.shard_map(
        grads,
        mesh=mesh,
        in_specs=placed,
        out_specs=(
            P(("dp", "expert"), None),
            P("expert", None, "dp"),
            P("expert", "dp", None),
            P(),
        ),
        check_vma=False,
    )
```

```python
import jax
import jax.numpy as jnp
from jax import lax
from jax.sharding import PartitionSpec as P


SLOT = 2


def dot_rows(left, right):
    return lax.dot_general(
        left, right, (((0,), (0,)), ((), ())), preferred_element_type=jnp.float32
    )


def dot_cols(left, right):
    return lax.dot_general(
        left, right, (((1,), (1,)), ((), ())), preferred_element_type=jnp.float32
    )


def dot_plain(left, right):
    return jnp.dot(left, right, preferred_element_type=jnp.float32)


def split_bf16(values, pieces):
    parts = []
    rest = values
    for _ in range(pieces):
        head = lax.reduce_precision(rest, 8, 7)
        parts.append(head.astype(jnp.bfloat16))
        rest = rest - head
    return parts


def one_hot(index, width):
    lanes = lax.broadcasted_iota(jnp.int32, (index.shape[0], width), 1)
    return (lanes == index[:, None]).astype(jnp.bfloat16)


def grads(tokens, cotangent, counts, picks, router, w_in, w_out):
    experts = lax.axis_size("expert")
    groups = lax.axis_size("dp")
    me = lax.axis_index("expert")
    tok_count, width = tokens.shape
    plan = picks[0]
    cap = plan.shape[1]
    hidden = w_in.shape[2]
    block_in = w_in[0]
    block_out = w_out[0]

    low = me * tok_count
    inside = (plan >= low) & (plan < low + tok_count)
    held = jnp.sum(inside.astype(jnp.int32), axis=1)
    first = jnp.min(jnp.where(inside, plan, low + tok_count), axis=1) - low
    last = jnp.max(jnp.where(inside, plan, low - 1), axis=1) - low
    slot_a = jnp.where(held > 0, first, -1)
    slot_b = jnp.where(held > 1, last, -1)

    weight = jnp.maximum(counts, 1).astype(jnp.float32)
    scaled = (cotangent.astype(jnp.float32) / weight[:, None]).astype(jnp.bfloat16)
    none = jnp.full_like(slot_a, -1)
    pick_x = one_hot(jnp.stack([slot_a, slot_b, none, none], axis=1).reshape(-1), tok_count)
    pick_dy = one_hot(jnp.stack([none, none, slot_a, slot_b], axis=1).reshape(-1), tok_count)
    send = dot_plain(pick_x, tokens) + dot_plain(pick_dy, scaled)
    send = send.astype(jnp.bfloat16).reshape(experts, 2 * SLOT, width)
    recv = lax.all_to_all(send, "expert", split_axis=0, concat_axis=0, tiled=True)
    recv = recv.reshape(experts * 2 * SLOT, width)

    mine = lax.dynamic_index_in_dim(plan, me, 0, keepdims=False)
    owner = mine // tok_count
    rank = jnp.concatenate(
        [jnp.zeros((1,), jnp.int32), (owner[1:] == owner[:-1]).astype(jnp.int32)]
    )
    place_x = owner * (2 * SLOT) + rank
    pack = one_hot(jnp.concatenate([place_x, place_x + SLOT]), experts * 2 * SLOT)
    slab = dot_plain(pack, recv).astype(jnp.bfloat16)
    swap = [(i, i ^ 1) for i in range(groups)]
    partner_in = lax.ppermute(block_in, "dp", swap)
    partner_out = lax.ppermute(block_out, "dp", swap)
    both_in = jnp.concatenate([block_in, partner_in], axis=1)
    both_out = jnp.concatenate([block_out, partner_out])
    both_in, both_out = lax.optimization_barrier((both_in, both_out))

    chips = groups // 2
    here = lax.axis_index("dp") // 2
    shape = (chips, cap, width)
    blocks_x = jnp.zeros(shape, jnp.bfloat16)
    blocks_dy = jnp.zeros(shape, jnp.bfloat16)
    up = down = slab
    for step in range(chips // 2 + 1):
        arrived = []
        if step == 0:
            arrived.append((slab, here))
        else:
            up = lax.ppermute(up, "dp", [(i, (i + 2) % groups) for i in range(groups)])
            arrived.append((up, (here - step) % chips))
            if step < chips // 2:
                down = lax.ppermute(down, "dp", [(i, (i - 2) % groups) for i in range(groups)])
                arrived.append((down, (here + step) % chips))
        for block, spot in arrived:
            blocks_x = lax.dynamic_update_slice(blocks_x, block[None, :cap], (spot, 0, 0))
            blocks_dy = lax.dynamic_update_slice(blocks_dy, block[None, cap:], (spot, 0, 0))
    rows_x = blocks_x.reshape(chips * cap, width)
    rows_dy = blocks_dy.reshape(chips * cap, width)

    router_parts = split_bf16(router, 3)
    router_wide = jnp.concatenate(router_parts, axis=1)
    router_back = jnp.concatenate([router_parts[0], router_parts[0], router_parts[1]], axis=1)
    mark = (lax.broadcasted_iota(jnp.int32, (1, experts), 1) == me).astype(jnp.float32)

    logit_parts = dot_plain(rows_x, router_wide)
    logits = (
        logit_parts[:, 2 * experts :] + logit_parts[:, experts : 2 * experts]
    ) + logit_parts[:, :experts]
    prob = jax.nn.softmax(logits, axis=-1)
    gate = jnp.sum(prob * mark, axis=-1, keepdims=True)
    pre = dot_plain(rows_x, both_in)
    cdf = 0.5 * (1.0 + lax.erf(pre * 0.7071067811865476))
    slope = cdf + pre * jnp.exp(-0.5 * pre * pre) * 0.3989422804014327
    act = (pre * cdf).astype(jnp.bfloat16)
    dy_hidden = dot_cols(rows_dy, both_out)
    gate_part = jnp.sum(act.astype(jnp.float32) * dy_hidden, axis=-1, keepdims=True)
    pre_grad = (gate * dy_hidden * slope).astype(jnp.bfloat16)
    gated = (gate * act.astype(jnp.float32)).astype(jnp.bfloat16)

    share_hi, share_lo = split_bf16((gate_part * gate) * (mark - prob), 2)

    tiles = width // 128
    deal = experts * tiles // groups
    core = lax.axis_index("dp") % 2
    row_id = jnp.arange(chips * cap, dtype=jnp.int32)
    router_part = dot_rows(share_hi, rows_x) + dot_rows(share_lo, rows_x)
    router_part = router_part.astype(jnp.bfloat16)
    router_part = jnp.concatenate(
        [router_part[:, 128 * tile : 128 * (tile + 1)] for tile in range(tiles)]
    )

    def dealt(side):
        group, spot = 2 * (row_id // cap) + side, row_id % cap
        unit = spot % tiles * experts + SLOT * group + spot // tiles
        pick = one_hot(jnp.where(spot < deal, unit, -1), experts * tiles)
        return dot_plain(pick, router_part)

    partner_extra = lax.ppermute(dealt(1 - core).astype(jnp.bfloat16), "dp", swap)
    extra = (dealt(core) + partner_extra.astype(jnp.float32)).astype(jnp.bfloat16)

    left = jnp.concatenate([share_hi, share_lo, share_hi], axis=1)
    rows = (dot_cols(pre_grad, both_in) + dot_cols(left, router_back)).astype(jnp.bfloat16)
    rows = jnp.concatenate([rows, extra], axis=1).reshape(chips, cap, width + 128)
    columns = [[i for i in range(groups) if i % 2 == side] for side in range(2)]
    pieces = lax.all_to_all(
        rows,
        "dp",
        split_axis=0,
        concat_axis=0,
        axis_index_groups=columns,
        tiled=True,
    )
    router_rows = jnp.sum(pieces[:, :deal, width:].astype(jnp.float32), axis=0)
    router_rows = router_rows.reshape(SLOT, width)

    partner_in = dot_rows(rows_x, pre_grad[:, hidden:]).astype(jnp.bfloat16)
    partner_out = dot_rows(gated[:, hidden:], rows_dy).astype(jnp.bfloat16)
    partner_in = lax.ppermute(partner_in, "dp", swap)
    partner_out = lax.ppermute(partner_out, "dp", swap)
    grad_in = dot_rows(rows_x, pre_grad[:, :hidden]) + partner_in.astype(jnp.float32)
    grad_out = dot_rows(gated[:, :hidden], rows_dy) + partner_out.astype(jnp.float32)
    grad_in, grad_out = grad_in.astype(jnp.bfloat16), grad_out.astype(jnp.bfloat16)

    slot = lax.broadcasted_iota(jnp.int32, (experts * 2 * SLOT, 1), 0) % (2 * SLOT)
    spread = one_hot(jnp.tile(place_x, chips), experts * 2 * SLOT)
    back_rows = dot_rows(spread, pieces[:, :, :width].reshape(chips * cap, width))
    for part in range(SLOT):
        back_rows += jnp.where(slot == SLOT + part, router_rows[part : part + 1], 0.0)
    ret = lax.all_to_all(
        back_rows.astype(jnp.bfloat16).reshape(experts, 2 * SLOT, width),
        "expert",
        split_axis=0,
        concat_axis=0,
        tiled=True,
    )
    router_rows = jnp.sum(ret[:, SLOT:].astype(jnp.float32), axis=0)
    grad_tokens = dot_rows(pick_x, ret.reshape(experts * 2 * SLOT, width)).astype(jnp.bfloat16)
    router_rows = router_rows.astype(jnp.bfloat16)
    router_rows = jnp.broadcast_to(router_rows[None], (groups, SLOT, width))
    router_rows = lax.all_to_all(router_rows, "dp", split_axis=0, concat_axis=0, tiled=True)
    grad_router = router_rows.reshape(experts, width).astype(jnp.float32).T
    return grad_tokens, grad_in[None], grad_out[None], grad_router


def solution(mesh):
    placed = (
        P(("dp", "expert"), None),
        P(("dp", "expert"), None),
        P(("dp", "expert")),
        P("dp", None, None),
        P(),
        P("expert", None, "dp"),
        P("expert", "dp", None),
    )
    return jax.shard_map(
        grads,
        mesh=mesh,
        in_specs=placed,
        out_specs=(
            P(("dp", "expert"), None),
            P("expert", None, "dp"),
            P("expert", "dp", None),
            P(),
        ),
        check_vma=False,
    )
```
